32 devices in a mesh: grp: 2 (over x), seqa: 8 (over z, y), seqb: 2 (over core).
Axes of the slice: x: 2, y: 2, z: 4, core: 2. Of those that a mesh axis runs over, the one named last changes fastest.
Arguments:
- inputs: bfloat16 [128, 256, 768], P(('grp', 'seqa', 'seqb')), parts along dimension 0, may hold values from -6 to 6
- out_grad: bfloat16 [128, 256, 768], P(('grp', 'seqa', 'seqb')), parts along dimension 0, may hold values from -24 to 24
- w_query: bfloat16 [768, 768], replicated, may hold values from -0.21875 to 0.21875
- w_key: bfloat16 [768, 768], replicated, may hold values from -0.21875 to 0.21875
- w_value: bfloat16 [768, 768], replicated, may hold values from -0.21875 to 0.21875
- w_output: bfloat16 [768, 768], replicated, may hold values from -0.21875 to 0.21875
- saved_probs: float32 [512, 12, 256], P('grp'), parts along dimension 0, may hold values from 0 to 1, as said below
Outputs:
- input_grad: float32 [128, 256, 768], P(('grp', 'seqa', 'seqb')), parts along dimension 0
The draws below stay inside these ranges and needn't reach their ends.
There are 2 independent parts, one for each index of `grp`. The reference program is written for one: setup_inputs(seed, part) draws one part's arguments, and reference() takes and returns one part's arrays. A program takes and returns all parts, laid end to end along the dimension named above; an argument that names none is the same for every part. Nothing has to cross between parts.
Inputs may be any that keep to these rules, and one draw needn't show every extreme that they name: `saved_probs`: for every query residue and head, the 256 weights over key residues are positive and sum to one.
All inputs are finite; a program needn't handle non-finite values.
Results may differ from the reference program's by a relative error of at most 0.018.
Values may be sent and summed in bfloat16 or wider, within the bound.
No kernel may reach another device: no remote copies, remote signals or barrier semaphores. Data moves between devices by JAX's collectives and lax.ppermute only.
A program may use at most 64 MiB of HBM per device.

```python
import math
import jax
import jax.numpy as jnp
from jax import lax

D = 768
H = 12
E = 64
L = 256
SEQ_DEV = 4
SEQS = 64


def draw_saved_probs(key, part):
    head_key = jax.random.fold_in(key, 11)
    logit_key = jax.random.fold_in(key, 23)
    spread = jnp.exp(jax.random.uniform(head_key, (1, H, 1), jnp.float32, math.log(0.5), math.log(2.5)))
    base = jax.random.normal(logit_key, (L, H, L), jnp.float32)
    return jax.nn.softmax(spread * base, axis=-1)


def level_of(own_key, extent, split, least, high):
    gain, own = 1.0, jax.random.fold_in(own_key, 6)
    for position, parts in split:
        heights = jnp.exp(jax.random.uniform(jax.random.fold_in(own, position), (parts,), jnp.float32, least / len(split), high / len(split)))
        gain = gain * jnp.repeat(heights, extent[position] // parts).reshape([-1 if axis == position else 1 for axis in range(len(extent))])
    return gain


def gaussian(rng, shape, width, bound, split=(), kind=jnp.bfloat16):
    entries = width * jax.random.normal(rng, shape, jnp.float32)
    if split:
        entries = entries * level_of(rng, shape, split, -0.22, 0.18)
    return jnp.clip(entries, -bound, bound).astype(kind)


def setup_inputs(seed: int = 0, part: int = 0) -> dict:
    keys = jax.random.split(jax.random.key(seed), 8)
    part_keys = jax.random.split(jax.random.fold_in(keys[7], part), 8)
    inputs = gaussian(part_keys[0], (SEQS, L, D), 1.0, 6.0, ((0, 16),))
    out_grad = gaussian(part_keys[1], (SEQS, L, D), 4.0, 24.0, ((0, 16),))
    w_query = gaussian(keys[2], (D, D), D ** -0.5, 0.21875)
    w_key = gaussian(keys[3], (D, D), D ** -0.5, 0.21875)
    w_value = gaussian(keys[4], (D, D), D ** -0.5, 0.21875)
    w_output = gaussian(keys[5], (D, D), D ** -0.5, 0.21875)
    saved_probs = draw_saved_probs(jax.random.fold_in(jax.random.fold_in(keys[7], part), 71), part)
    return dict(inputs=inputs, out_grad=out_grad, w_query=w_query, w_key=w_key, w_value=w_value, w_output=w_output, saved_probs=saved_probs)


def split_heads(flat_rows):
    return flat_rows.reshape(SEQ_DEV, L, H, E)


def project(block, weight):
    flat_rows = jnp.dot(block.reshape(-1, D), weight, preferred_element_type=jnp.float32)
    return split_heads(flat_rows.astype(jnp.bfloat16))


def back_project(block, weight):
    flat_rows = jnp.dot(block.reshape(-1, D), weight.T, preferred_element_type=jnp.float32)
    return split_heads(flat_rows.astype(jnp.bfloat16))


def reference(inputs, out_grad, w_query, w_key, w_value, w_output, saved_probs):
    blocks = SEQS // SEQ_DEV
    input_blocks = inputs.reshape(blocks, SEQ_DEV, L, D)
    grad_blocks = out_grad.reshape(blocks, SEQ_DEV, L, D)

    def map_term(total, pair):
        in_block, grad_block = pair
        values = project(in_block, w_value)
        attn_grad = back_project(grad_block, w_output)
        term = jnp.einsum("sihe,sjhe->ihj", attn_grad.astype(jnp.float32), values.astype(jnp.float32))
        return total + term, None

    map_grad, unused = lax.scan(map_term, jnp.zeros((L, H, L), jnp.float32), (input_blocks, grad_blocks))
    inner = jnp.sum(saved_probs * map_grad, axis=-1, keepdims=True)
    logit_grad = (saved_probs * (map_grad - inner)).astype(jnp.bfloat16)
    probs_low = saved_probs.astype(jnp.bfloat16)
    scale = (E * SEQS) ** -0.5
    logit_wide = logit_grad.astype(jnp.float32)
    probs_wide = probs_low.astype(jnp.float32)

    def per_block(pair):
        in_block, grad_block = pair
        queries = project(in_block, w_query).astype(jnp.float32)
        key_rows = project(in_block, w_key).astype(jnp.float32)
        attn_grad = back_project(grad_block, w_output).astype(jnp.float32)
        query_grad = (scale * jnp.einsum("ihj,sjhe->sihe", logit_wide, key_rows)).astype(jnp.bfloat16)
        key_grad = (scale * jnp.einsum("ihj,sihe->sjhe", logit_wide, queries)).astype(jnp.bfloat16)
        value_grad = jnp.einsum("ihj,sihe->sjhe", probs_wide, attn_grad).astype(jnp.bfloat16)
        total = jnp.dot(query_grad.reshape(-1, D), w_query.T, preferred_element_type=jnp.float32)
        total = total + jnp.dot(key_grad.reshape(-1, D), w_key.T, preferred_element_type=jnp.float32)
        total = total + jnp.dot(value_grad.reshape(-1, D), w_value.T, preferred_element_type=jnp.float32)
        return total.reshape(SEQ_DEV, L, D)

    result = lax.map(per_block, (input_blocks, grad_blocks))
    return result.reshape(SEQS, L, D)
```

```python
import functools

import jax
import jax.numpy as jnp
from jax import lax
from jax.experimental import pallas as pl
from jax.experimental.pallas import tpu as pltpu
from jax.sharding import PartitionSpec as P


F32 = jnp.float32
BF16 = jnp.bfloat16
GROUP = 4


def dot_nn(a, b):
    return lax.dot_general(a, b, (((1,), (0,)), ((), ())), preferred_element_type=F32)


def dot_nt(a, b):
    return lax.dot_general(a, b, (((1,), (1,)), ((), ())), preferred_element_type=F32)


def dot_tn(a, b):
    return lax.dot_general(a, b, (((0,), (0,)), ((), ())), preferred_element_type=F32)


def gather_head(rows, seqs, head, size):
    n = rows.shape[0] // seqs
    lanes = slice(head * size, (head + 1) * size)
    return jnp.concatenate([rows[s * n : (s + 1) * n, lanes] for s in range(seqs)], axis=1)


def spread_heads(parts, seqs, size):
    return [
        jnp.concatenate([p[:, s * size : (s + 1) * size] for p in parts], axis=1)
        for s in range(seqs)
    ]


def resident(shape):
    return pl.BlockSpec(shape, lambda *_: (0,) * len(shape), pipeline_mode=pl.Buffered(1))


def radices_of(count):
    out = []
    while count > 1:
        r = 4 if count % 4 == 0 else 2
        assert count % r == 0
        out.append(r)
        count //= r
    return tuple(out)


def position_of(mask, radices):
    pos, shift = 0, 0
    for r in radices:
        bits = r.bit_length() - 1
        pos = pos * r + ((mask >> shift) & (r - 1))
        shift += bits
    return pos


def map_kernel(dims, radices, which, with_values, sc, og, w_out, *refs):
    seqs, length, heads, size, cores, others, rows = dims
    if with_values:
        x, w_val, m_out, a_out, v_all = refs
    else:
        v_all, m_out, a_out = refs
    core = sc[0] if which == 0 else 1 - sc[0]
    half = length // cores
    start = pl.multiple_of(core * half, half)
    width = og.shape[-1]
    og_rows = og[:, pl.ds(start, half), :].reshape(seqs * half, width)
    a4 = dot_nt(og_rows, w_out[...]).astype(BF16)
    if with_values:
        v4 = dot_nn(x[...].reshape(seqs * length, width), w_val[...]).astype(BF16)
    for h in range(GROUP):
        a = gather_head(a4, seqs, h, size)
        a_out[h] = a
        if with_values:
            v = gather_head(v4, seqs, h, size)
            v_all[h] = v
        else:
            v = v_all[h]
        m = dot_nt(a, v).astype(BF16)
        for q in range(others):
            pos = position_of(sc[1] ^ q, radices)
            m_out[pos, h] = m[q * rows : (q + 1) * rows]


def mid_kernel(dims, sc, x, a_own, a_other, probs, w_q, w_k, w_v, q_out, k_out, o_out):
    seqs, length, heads, size, cores, others, rows = dims
    width = x.shape[-1]
    half = length // cores
    flat = x[...].reshape(seqs * length, width)
    q4 = dot_nn(flat, w_q[...]).astype(BF16)
    k4 = dot_nn(flat, w_k[...]).astype(BF16)
    own = pl.multiple_of(sc[0] * half, half)
    other = pl.multiple_of((1 - sc[0]) * half, half)
    parts = []
    for h in range(GROUP):
        q_out[h] = gather_head(q4, seqs, h, size)
        k_out[h] = gather_head(k4, seqs, h, size)
        p_own = probs[h, pl.ds(own, half), :].astype(BF16)
        p_other = probs[h, pl.ds(other, half), :].astype(BF16)
        vg = dot_tn(p_own, a_own[h]) + dot_tn(p_other, a_other[h])
        parts.append(vg.astype(BF16))
    first = pl.program_id(0) == 0
    for s, block in enumerate(spread_heads(parts, seqs, size)):
        term = dot_nt(block, w_v[...])

        @pl.when(first)
        def _():
            o_out[s] = term

        @pl.when(jnp.logical_not(first))
        def _():
            o_out[s] += term


def post_kernel(dims, radices, sc, *refs):
    seqs, length, heads, size, cores, others, rows = dims
    first = radices[0]
    own, other = refs[:first], refs[first : 2 * first]
    q_all, k_all, w_q, w_k, o_v, out, logit, q_grad, k_grad = refs[2 * first :]
    scale = (size * seqs * cores * others) ** -0.5
    half = length // cores
    inner = others // first

    @pl.when(pl.program_id(0) == 0)
    def _():
        for which, parts in ((0, own), (1, other)):
            core = sc[0] if which == 0 else 1 - sc[0]
            for mask in range(others):
                pos = position_of(mask, radices)
                m, rest = pos // inner, pos % inner
                q = sc[1] ^ mask
                start = pl.multiple_of(core * half + q * rows, rows)
                for h in range(heads):
                    logit[h, pl.ds(start, rows), :] = parts[m][rest, h]
        for g in range(heads // GROUP):
            qs, ks = [], []
            for h in range(g * GROUP, (g + 1) * GROUP):
                lg = logit[h]
                qs.append((scale * dot_nn(lg, k_all[h])).astype(BF16))
                ks.append((scale * dot_tn(lg, q_all[h])).astype(BF16))
            lanes = slice(g * GROUP * size, (g + 1) * GROUP * size)
            for s, block in enumerate(spread_heads(qs, seqs, size)):
                q_grad[s, :, lanes] = block
            for s, block in enumerate(spread_heads(ks, seqs, size)):
                k_grad[s, :, lanes] = block

    s = pl.program_id(0)
    out[0] = o_v[0] + dot_nt(q_grad[s], w_q[...]) + dot_nt(k_grad[s], w_k[...])


def exchange(x, axis, mask):
    count = lax.axis_size(axis)
    return lax.ppermute(x, axis, [(i, i ^ mask) for i in range(count)])


def cost(flops, nbytes):
    return pl.CostEstimate(flops=int(flops), bytes_accessed=int(nbytes), transcendentals=0)


def local(inputs, out_grad, w_query, w_key, w_value, w_output, saved_probs):
    seqs, length, width = inputs.shape
    heads = saved_probs.shape[1]
    size = width // heads
    cores, others = lax.axis_size("seqb"), lax.axis_size("seqa")
    rows = length // (cores * others)
    dims = (seqs, length, heads, size, cores, others, rows)
    radices = radices_of(others)
    half = length // cores
    lanes = seqs * size
    core, chip = lax.axis_index("seqb"), lax.axis_index("seqa")
    sc = jnp.stack([core, chip]).astype(jnp.int32)
    probs = jnp.swapaxes(saved_probs, 0, 1)
    params = pltpu.CompilerParams(dimension_semantics=("arbitrary",))
    proj = 2 * seqs * length * width * width
    mapf = 2 * heads * length * length * lanes
    col = pl.BlockSpec((width, GROUP * size), lambda g, s: (0, g))
    row = pl.BlockSpec((GROUP * size, width), lambda g, s: (g, 0))
    head_spec = lambda n, m: pl.BlockSpec((GROUP, n, m), lambda g, s: (g, 0, 0))
    m_spec = pl.BlockSpec((others, GROUP, rows, length), lambda g, s: (0, g, 0, 0))
    m_shape = jax.ShapeDtypeStruct((others, heads, rows, length), BF16)
    a_shape = jax.ShapeDtypeStruct((heads, half, lanes), BF16)
    v_shape = jax.ShapeDtypeStruct((heads, length, lanes), BF16)

    with jax.named_scope("map_send"):
        m_send, a_other, v_all = pl.pallas_call(
            functools.partial(map_kernel, dims, radices, 1, True),
            grid_spec=pltpu.PrefetchScalarGridSpec(
                num_scalar_prefetch=1,
                grid=(heads // GROUP,),
                in_specs=[resident(out_grad.shape), row, resident(inputs.shape), col],
                out_specs=[m_spec, head_spec(half, lanes), head_spec(length, lanes)],
            ),
            out_shape=[m_shape, a_shape, v_shape],
            compiler_params=params,
            cost_estimate=cost(1.5 * proj + mapf / 2, 8e6),
            name="map_send",
        )(sc, out_grad, w_output, inputs, w_value)
    m_recv = exchange(m_send, "seqb", 1)
    with jax.named_scope("map_keep"):
        m_keep, a_own = pl.pallas_call(
            functools.partial(map_kernel, dims, radices, 0, False),
            grid_spec=pltpu.PrefetchScalarGridSpec(
                num_scalar_prefetch=1,
                grid=(heads // GROUP,),
                in_specs=[resident(out_grad.shape), row, head_spec(length, lanes)],
                out_specs=[m_spec, head_spec(half, lanes)],
            ),
            out_shape=[m_shape, a_shape],
            compiler_params=params,
            cost_estimate=cost(0.5 * proj + mapf / 2, 5e6),
            name="map_keep",
        )(sc, out_grad, w_output, v_all)

    p_rows = lax.dynamic_slice_in_dim(probs, core * half + chip * rows, rows, 1)

    total = (m_keep.astype(F32) + m_recv.astype(F32)).reshape(
        radices + (heads, rows, length)
    )
    shift = 0
    for r in radices:
        terms = [
            exchange(total[m].astype(BF16), "seqa", m << shift) for m in range(1, r)
        ]
        total = functools.reduce(lambda t, u: t + u.astype(F32), terms, total[0])
        shift += r.bit_length() - 1
    inner = jnp.sum(p_rows * total, axis=-1, keepdims=True)
    logit = (p_rows * (total - inner)).astype(BF16)

    with jax.named_scope("mid"):
        q_all, k_all, o_v = pl.pallas_call(
            functools.partial(mid_kernel, dims),
            grid_spec=pltpu.PrefetchScalarGridSpec(
                num_scalar_prefetch=1,
                grid=(heads // GROUP,),
                in_specs=[
                    resident(inputs.shape),
                    head_spec(half, lanes),
                    head_spec(half, lanes),
                    head_spec(length, length),
                    col,
                    col,
                    col,
                ],
                out_specs=[
                    head_spec(length, lanes),
                    head_spec(length, lanes),
                    resident(inputs.shape),
                ],
            ),
            out_shape=[v_shape, v_shape, jax.ShapeDtypeStruct(inputs.shape, F32)],
            compiler_params=params,
            cost_estimate=cost(3 * proj + mapf, 16e6),
            name="mid",
        )(sc, inputs, a_own, a_other, probs, w_query, w_key, w_value)

    parts = [logit]
    for r in radices[::-1]:
        block = jnp.stack(parts) if len(parts) > 1 else parts[0][None]
        if block.ndim > 4:
            block = block.reshape((-1,) + block.shape[2:])
        shift -= r.bit_length() - 1
        parts = [block] + [exchange(block, "seqa", m << shift) for m in range(1, r)]
    crossed = [exchange(p, "seqb", 1) for p in parts]

    part_spec = resident(parts[0].shape)
    with jax.named_scope("post"):
        return pl.pallas_call(
            functools.partial(post_kernel, dims, radices),
            grid_spec=pltpu.PrefetchScalarGridSpec(
                num_scalar_prefetch=1,
                grid=(seqs,),
                in_specs=[part_spec] * (2 * radices[0])
                + [resident(v_shape.shape)] * 2
                + [resident(w_query.shape)] * 2
                + [pl.BlockSpec((1, length, width), lambda s, sc: (s, 0, 0))],
                out_specs=pl.BlockSpec((1, length, width), lambda s, sc: (s, 0, 0)),
                scratch_shapes=[
                    pltpu.VMEM((heads, length, length), BF16),
                    pltpu.VMEM((seqs, length, width), BF16),
                    pltpu.VMEM((seqs, length, width), BF16),
                ],
            ),
            out_shape=jax.ShapeDtypeStruct(inputs.shape, F32),
            compiler_params=params,
            cost_estimate=cost(2 * proj + 2 * mapf, 12e6),
            name="post",
        )(sc, *parts, *crossed, q_all, k_all, w_query, w_key, o_v)


def solution(mesh):
    placed = (
        P(("grp", "seqa", "seqb"), None, None),
        P(("grp", "seqa", "seqb"), None, None),
        P(),
        P(),
        P(),
        P(),
        P("grp", None, None),
    )
    return jax.shard_map(
        local,
        mesh=mesh,
        in_specs=placed,
        out_specs=P(("grp", "seqa", "seqb"), None, None),
        check_vma=False,
    )
```

```python
import functools

import jax
import jax.numpy as jnp
from jax import lax
from jax.experimental import pallas as pl
from jax.experimental.pallas import tpu as pltpu
from jax.sharding import PartitionSpec as P


F32 = jnp.float32
BF16 = jnp.bfloat16
VMEM_LIMIT = 14 << 20
SEND_LIMIT = 14 << 20
GROUP = 4


def dot_nn(a, b):
    return lax.dot_general(a, b, (((1,), (0,)), ((), ())), preferred_element_type=F32)


def dot_nt(a, b):
    return lax.dot_general(a, b, (((1,), (1,)), ((), ())), preferred_element_type=F32)


def dot_tn(a, b):
    return lax.dot_general(a, b, (((0,), (0,)), ((), ())), preferred_element_type=F32)


def gather_head(rows, seqs, head, size):
    n = rows.shape[0] // seqs
    lanes = slice(head * size, (head + 1) * size)
    return jnp.concatenate([rows[s * n : (s + 1) * n, lanes] for s in range(seqs)], axis=1)


def spread_heads(parts, seqs, size):
    return [
        jnp.concatenate([p[:, s * size : (s + 1) * size] for p in parts], axis=1)
        for s in range(seqs)
    ]


def radices_of(count):
    out = []
    while count > 1:
        r = 4 if count % 4 == 0 else 2
        assert count % r == 0
        out.append(r)
        count //= r
    return tuple(out)


def position_of(mask, radices):
    pos, shift = 0, 0
    for r in radices:
        bits = r.bit_length() - 1
        pos = pos * r + ((mask >> shift) & (r - 1))
        shift += bits
    return pos


def fetch(pairs, sems):
    copies = [pltpu.make_async_copy(a, b, sems.at[i]) for i, (a, b) in enumerate(pairs)]
    for c in copies:
        c.start()
    return copies


def store_map(m, h, m_out, chip, others, rows, radices):
    for q in range(others):
        m_out[position_of(chip ^ q, radices), h] = m[q * rows : (q + 1) * rows]


def map_send_kernel(
    dims, radices, sc, x_hbm, wv_hbm, og_hbm, wo_hbm, m_out, a_out, v_out, x, og, wo, wv, sems
):
    seqs, length, heads, size, cores, others, rows = dims
    copies = fetch([(x_hbm, x), (wv_hbm, wv), (wo_hbm, wo), (og_hbm, og)], sems)
    width = x.shape[-1]
    half = length // cores
    start = pl.multiple_of((1 - sc[0]) * half, half)
    copies[0].wait()
    copies[1].wait()
    flat = x[...].reshape(seqs * length, width)
    for g in range(heads // GROUP):
        lanes = slice(g * GROUP * size, (g + 1) * GROUP * size)
        v4 = dot_nn(flat, wv[:, lanes]).astype(BF16)
        for h in range(GROUP):
            v_out[g * GROUP + h] = gather_head(v4, seqs, h, size)
    copies[2].wait()
    copies[3].wait()
    og_rows = og[:, pl.ds(start, half), :].reshape(seqs * half, width)
    for g in range(heads // GROUP):
        a4 = dot_nt(og_rows, wo[g * GROUP * size : (g + 1) * GROUP * size]).astype(BF16)
        for h in range(GROUP):
            a = gather_head(a4, seqs, h, size)
            a_out[g * GROUP + h] = a
            m = dot_nt(a, v_out[g * GROUP + h]).astype(BF16)
            store_map(m, g * GROUP + h, m_out, sc[1], others, rows, radices)


def map_keep_kernel(dims, radices, sc, og, wo, v_all, m_out, a_out):
    seqs, length, heads, size, cores, others, rows = dims
    width = og.shape[-1]
    half = length // cores
    start = pl.multiple_of(sc[0] * half, half)
    og_rows = og[:, pl.ds(start, half), :].reshape(seqs * half, width)
    for g in range(heads // GROUP):
        a4 = dot_nt(og_rows, wo[g * GROUP * size : (g + 1) * GROUP * size]).astype(BF16)
        for h in range(GROUP):
            a = gather_head(a4, seqs, h, size)
            a_out[g * GROUP + h] = a
            m = dot_nt(a, v_all[g * GROUP + h]).astype(BF16)
            store_map(m, g * GROUP + h, m_out, sc[1], others, rows, radices)


def value_kernel(dims, sc, a_own, a_other, wv, probs, o_out, p_out):
    seqs, length, heads, size, cores, _, rows = dims
    half = length // cores
    own = pl.multiple_of(sc[0] * half, half)
    other = pl.multiple_of((1 - sc[0]) * half, half)
    p_out[...] = probs[:, pl.ds(pl.multiple_of(own + sc[1] * rows, rows), rows), :]
    for g in range(heads // GROUP):
        lanes = slice(g * GROUP * size, (g + 1) * GROUP * size)
        parts = []
        for h in range(g * GROUP, (g + 1) * GROUP):
            p_own = probs[h, pl.ds(own, half), :].astype(BF16)
            p_other = probs[h, pl.ds(other, half), :].astype(BF16)
            vg = dot_tn(p_own, a_own[h]) + dot_tn(p_other, a_other[h])
            parts.append(vg.astype(BF16))
        for s, block in enumerate(spread_heads(parts, seqs, size)):
            term = dot_nt(block, wv[:, lanes])
            if g:
                o_out[s] += term
            else:
                o_out[s] = term


def query_key_kernel(dims, x, wq, wk, q_out, k_out):
    seqs, length, heads, size, _, _, _ = dims
    flat = x[...].reshape(seqs * length, x.shape[-1])
    for g in range(heads // GROUP):
        lanes = slice(g * GROUP * size, (g + 1) * GROUP * size)
        q4 = dot_nn(flat, wq[:, lanes]).astype(BF16)
        k4 = dot_nn(flat, wk[:, lanes]).astype(BF16)
        for h in range(GROUP):
            q_out[g * GROUP + h] = gather_head(q4, seqs, h, size)
            k_out[g * GROUP + h] = gather_head(k4, seqs, h, size)


def first_sum_kernel(radix, keep, recv, own_out, *outs):
    for m, out in zip(range(radix), (own_out,) + outs):
        total = keep[m].astype(F32) + recv[m].astype(F32)
        out[...] = total.astype(out.dtype)


def sum_kernel(radix, count, keep, *refs):
    terms, own_out, outs = refs[: count - 1], refs[count - 1], refs[count:]
    assert len(outs) == radix - 1
    for m, out in enumerate((own_out,) + outs):
        total = keep[m]
        for t in terms:
            total = total + t[m].astype(F32)
        out[...] = total.astype(out.dtype)


def softmax_kernel(p_rows, keep, *refs):
    terms, out = refs[:-1], refs[-1]
    total = keep[...]
    for t in terms:
        total = total + t[...].astype(F32)
    p = p_rows[...]
    inner = jnp.sum(p * total, axis=-1, keepdims=True)
    out[...] = (p * (total - inner)).astype(BF16)


def post_kernel(dims, radices, sc, *refs):
    seqs, length, heads, size, cores, others, rows = dims
    first = radices[0]
    own, other = refs[:first], refs[first : 2 * first]
    q_all, k_all, w_q, w_k, o_v, out_hbm, logit, q_grad, k_grad, out, sems = refs[2 * first :]
    scale = (size * seqs * cores * others) ** -0.5
    half = length // cores
    inner = others // first
    for which, parts in ((0, own), (1, other)):
        core = sc[0] if which == 0 else 1 - sc[0]
        for mask in range(others):
            pos = position_of(mask, radices)
            m, rest = pos // inner, pos % inner
            q = sc[1] ^ mask
            start = pl.multiple_of(core * half + q * rows, rows)
            for h in range(heads):
                logit[h, pl.ds(start, rows), :] = parts[m][rest, h]
    for g in range(heads // GROUP):
        qs, ks = [], []
        for h in range(g * GROUP, (g + 1) * GROUP):
            lg = logit[h]
            qs.append((scale * dot_nn(lg, k_all[h])).astype(BF16))
            ks.append((scale * dot_tn(lg, q_all[h])).astype(BF16))
        lanes = slice(g * GROUP * size, (g + 1) * GROUP * size)
        for s, block in enumerate(spread_heads(qs, seqs, size)):
            q_grad[s, :, lanes] = block
        for s, block in enumerate(spread_heads(ks, seqs, size)):
            k_grad[s, :, lanes] = block
    copies = []
    for s in range(seqs):
        out[s] = o_v[s] + dot_nt(q_grad[s], w_q[...]) + dot_nt(k_grad[s], w_k[...])
        copies.append(pltpu.make_async_copy(out.at[s], out_hbm.at[s], sems.at[s]))
        copies[-1].start()
    for c in copies:
        c.wait()


def exchange(x, axis, mask):
    count = lax.axis_size(axis)
    return lax.ppermute(x, axis, [(i, i ^ mask) for i in range(count)])


def cost(flops, nbytes):
    return pl.CostEstimate(flops=int(flops), bytes_accessed=int(nbytes), transcendentals=0)


def local(inputs, out_grad, w_query, w_key, w_value, w_output, saved_probs):
    seqs, length, width = inputs.shape
    heads = saved_probs.shape[1]
    size = width // heads
    cores, others = lax.axis_size("seqb"), lax.axis_size("seqa")
    rows = length // (cores * others)
    dims = (seqs, length, heads, size, cores, others, rows)
    radices = radices_of(others)
    half = length // cores
    lanes = seqs * size
    core, chip = lax.axis_index("seqb"), lax.axis_index("seqa")
    sc = jnp.stack([core, chip]).astype(jnp.int32)
    probs = jnp.swapaxes(saved_probs, 0, 1)
    params = pltpu.CompilerParams(vmem_limit_bytes=VMEM_LIMIT)
    proj = 2 * seqs * length * width * width
    mapf = 2 * heads * length * length * lanes
    smem = pl.BlockSpec(memory_space=pltpu.SMEM)
    vmem = pl.BlockSpec(memory_space=pltpu.VMEM)
    hbm = pl.BlockSpec(memory_space=pltpu.HBM)
    m_shape = jax.ShapeDtypeStruct((others, heads, rows, length), BF16)
    a_shape = jax.ShapeDtypeStruct((heads, half, lanes), BF16)
    v_shape = jax.ShapeDtypeStruct((heads, length, lanes), BF16)
    like = lambda a: jax.ShapeDtypeStruct(a.shape, a.dtype)

    m_send, a_other, v_all, x_in, og_in, wo_in, wv_in = pl.pallas_call(
        functools.partial(map_send_kernel, dims, radices),
        in_specs=[smem, hbm, hbm, hbm, hbm],
        out_specs=[vmem] * 7,
        out_shape=[m_shape, a_shape, v_shape, like(inputs), like(out_grad)]
        + [like(w_output), like(w_value)],
        scratch_shapes=[pltpu.SemaphoreType.DMA((4,))],
        compiler_params=pltpu.CompilerParams(vmem_limit_bytes=SEND_LIMIT),
        cost_estimate=cost(1.5 * proj + mapf / 2, 8e6),
        name="map_send",
    )(sc, *[pltpu.with_memory_space_constraint(a, pltpu.HBM) for a in (inputs, w_value, out_grad, w_output)])
    m_recv = exchange(m_send, "seqb", 1)
    m_keep, a_own = pl.pallas_call(
        functools.partial(map_keep_kernel, dims, radices),
        in_specs=[smem, vmem, vmem, vmem],
        out_specs=[vmem] * 2,
        out_shape=[m_shape, a_shape],
        compiler_params=params,
        cost_estimate=cost(0.5 * proj + mapf / 2, 5e6),
        name="map_keep",
    )(sc, og_in, wo_in, v_all)

    o_v, p_rows = pl.pallas_call(
        functools.partial(value_kernel, dims),
        in_specs=[smem] + [vmem] * 4,
        out_specs=[vmem] * 2,
        out_shape=[
            jax.ShapeDtypeStruct(inputs.shape, F32),
            jax.ShapeDtypeStruct((heads, rows, length), F32),
        ],
        compiler_params=params,
        cost_estimate=cost(proj + mapf, 8e6),
        name="value",
    )(sc, a_own, a_other, wv_in, probs)

    shape = lambda n: radices[n:] + (heads, rows, length)
    small = lambda kernel, outs: pl.pallas_call(
        kernel,
        out_specs=[vmem] * len(outs),
        out_shape=outs,
        compiler_params=pltpu.CompilerParams(vmem_limit_bytes=6 << 20),
        cost_estimate=cost(1e6, 1e6),
    )
    split = lambda n: [jax.ShapeDtypeStruct(shape(n + 1), F32)] + [
        jax.ShapeDtypeStruct(shape(n + 1), BF16)
    ] * (radices[n] - 1)
    keep, *sends = small(
        functools.partial(first_sum_kernel, radices[0]), split(0)
    )(m_keep.reshape(shape(0)), m_recv.reshape(shape(0)))
    shift = 0
    for n, r in enumerate(radices):
        terms = [exchange(x, "seqa", m << shift) for m, x in enumerate(sends, 1)]
        shift += r.bit_length() - 1
        if n + 1 < len(radices):
            keep, *sends = small(
                functools.partial(sum_kernel, radices[n + 1], r), split(n + 1)
            )(keep, *terms)
    (logit,) = small(
        softmax_kernel, [jax.ShapeDtypeStruct((heads, rows, length), BF16)]
    )(p_rows, keep, *terms)

    q_all, k_all = pl.pallas_call(
        functools.partial(query_key_kernel, dims),
        in_specs=[vmem] * 3,
        out_specs=[vmem] * 2,
        out_shape=[v_shape, v_shape],
        compiler_params=params,
        cost_estimate=cost(2 * proj, 6e6),
        name="query_key",
    )(x_in, w_query, w_key)

    parts = [logit]
    for n, r in list(enumerate(radices))[::-1]:
        block = jnp.stack(parts) if len(parts) > 1 else parts[0][None]
        if block.ndim > 4:
            block = block.reshape((-1,) + block.shape[2:])
        shift -= r.bit_length() - 1
        parts = [block] + [exchange(block, "seqa", m << shift) for m in range(1, r)]
    crossed = [exchange(p, "seqb", 1) for p in parts]

    return pl.pallas_call(
        functools.partial(post_kernel, dims, radices),
        in_specs=[smem] + [vmem] * (2 * radices[0] + 5),
        out_specs=hbm,
        scratch_shapes=[
            pltpu.VMEM((heads, length, length), BF16),
            pltpu.VMEM((seqs, length, width), BF16),
            pltpu.VMEM((seqs, length, width), BF16),
            pltpu.VMEM((seqs, length, width), F32),
            pltpu.SemaphoreType.DMA((seqs,)),
        ],
        out_shape=jax.ShapeDtypeStruct(inputs.shape, F32),
        compiler_params=params,
        cost_estimate=cost(2 * proj + 2 * mapf, 12e6),
        name="post",
    )(sc, *parts, *crossed, q_all, k_all, w_query, w_key, o_v)


def solution(mesh):
    placed = (
        P(("grp", "seqa", "seqb"), None, None),
        P(("grp", "seqa", "seqb"), None, None),
        P(),
        P(),
        P(),
        P(),
        P("grp", None, None),
    )

    return jax.shard_map(
        local,
        mesh=mesh,
        in_specs=placed,
        out_specs=P(("grp", "seqa", "seqb"), None, None),
        check_vma=False,
    )
```

```python
import functools

import jax
import jax.numpy as jnp
from jax import lax
from jax.experimental import pallas as pl
from jax.experimental.pallas import tpu as pltpu
from jax.sharding import PartitionSpec as P


F32 = jnp.float32
BF16 = jnp.bfloat16
VMEM_LIMIT = 14 << 20
FIRST_PART = 0.67
GROUP = 4


def dot_nn(a, b):
    return lax.dot_general(a, b, (((1,), (0,)), ((), ())), preferred_element_type=F32)


def dot_nt(a, b):
    return lax.dot_general(a, b, (((1,), (1,)), ((), ())), preferred_element_type=F32)


def dot_tn(a, b):
    return lax.dot_general(a, b, (((0,), (0,)), ((), ())), preferred_element_type=F32)


def gather_head(rows, seqs, head, size):
    n = rows.shape[0] // seqs
    lanes = slice(head * size, (head + 1) * size)
    return jnp.concatenate([rows[s * n : (s + 1) * n, lanes] for s in range(seqs)], axis=1)


def spread_heads(parts, seqs, size):
    return [
        jnp.concatenate([p[:, s * size : (s + 1) * size] for p in parts], axis=1)
        for s in range(seqs)
    ]


def radices_of(count):
    out = []
    while count > 1:
        r = 4 if count % 4 == 0 else 2
        assert count % r == 0
        out.append(r)
        count //= r
    return tuple(out)


def position_of(mask, radices):
    pos, shift = 0, 0
    for r in radices:
        bits = r.bit_length() - 1
        pos = pos * r + ((mask >> shift) & (r - 1))
        shift += bits
    return pos


def fetch(pairs, sems):
    copies = [pltpu.make_async_copy(a, b, sems.at[i]) for i, (a, b) in enumerate(pairs)]
    for c in copies:
        c.start()
    return copies


def store_map(m, h, m_out, chip, others, rows, radices):
    for q in range(others):
        m_out[position_of(chip ^ q, radices), h] = m[q * rows : (q + 1) * rows]


def groups_of(count):
    return [(g, min(g + GROUP, count)) for g in range(0, count, GROUP)]


def value_rows(x, wv, v_out, first, dims):
    seqs, length, _, size, _, _, _ = dims
    flat = x[...].reshape(seqs * length, x.shape[-1])
    for a, b in groups_of(v_out.shape[0]):
        v4 = dot_nn(flat, wv[:, (first + a) * size : (first + b) * size]).astype(BF16)
        for h in range(b - a):
            v_out[a + h] = gather_head(v4, seqs, h, size)


def attn_rows(og, wo, a_out, first, dims):
    seqs, length, _, size, _, _, _ = dims
    flat = og[...].reshape(seqs * length, og.shape[-1])
    for a, b in groups_of(a_out.shape[0]):
        a4 = dot_nt(flat, wo[(first + a) * size : (first + b) * size]).astype(BF16)
        for h in range(b - a):
            a_out[a + h] = gather_head(a4, seqs, h, size)


def map_rows(core, chip, a_all, v_all, m_out, dims, radices):
    _, length, _, _, cores, others, rows = dims
    half = length // cores
    start = pl.multiple_of(core * half, half)
    for h in range(v_all.shape[0]):
        m = dot_nt(a_all[h, pl.ds(start, half), :], v_all[h]).astype(BF16)
        store_map(m, h, m_out, chip, others, rows, radices)


def first_map_kernel(
    dims, radices, sc, x_hbm, wv_hbm, og_hbm, wo_hbm, m_out, a_out, v_out, x, og, wo, wv, sems
):
    copies = fetch([(x_hbm, x), (wv_hbm, wv), (wo_hbm, wo), (og_hbm, og)], sems)
    copies[0].wait()
    copies[1].wait()
    value_rows(x, wv, v_out, 0, dims)
    copies[2].wait()
    copies[3].wait()
    attn_rows(og, wo, a_out, 0, dims)
    map_rows(1 - sc[0], sc[1], a_out, v_out, m_out, dims, radices)


def map_send_kernel(dims, radices, first, sc, x, wv, og, wo, m_out, a_out, v_out):
    value_rows(x, wv, v_out, first, dims)
    attn_rows(og, wo, a_out, first, dims)
    map_rows(1 - sc[0], sc[1], a_out, v_out, m_out, dims, radices)


def map_keep_kernel(dims, radices, sc, a_all, v_all, m_out):
    map_rows(sc[0], sc[1], a_all, v_all, m_out, dims, radices)


def value_kernel(dims, chunks, sc, *refs):
    seqs, length, _, size, _, others, rows = dims
    a_refs, (wv, probs, o_out), p_outs = (
        refs[: len(chunks)],
        refs[len(chunks) : len(chunks) + 3],
        refs[len(chunks) + 3 : -1],
    )
    v_grad = refs[-1]
    mine = pl.ds(pl.multiple_of((sc[0] * others + sc[1]) * rows, rows), rows)
    for (first, n), a_all, p_out in zip(chunks, a_refs, p_outs):
        p_out[...] = probs[first : first + n, mine, :]
        for a, b in groups_of(n):
            parts = [
                dot_tn(probs[first + h].astype(BF16), a_all[h]).astype(BF16)
                for h in range(a, b)
            ]
            lanes = slice((first + a) * size, (first + b) * size)
            for s, block in enumerate(spread_heads(parts, seqs, size)):
                v_grad[s * length : (s + 1) * length, lanes] = block
    o_out[...] = dot_nt(v_grad[...], wv[...]).reshape(o_out.shape)


def query_key_kernel(dims, x, wq, wk, q_out, k_out):
    seqs, length, heads, size, _, _, _ = dims
    flat = x[...].reshape(seqs * length, x.shape[-1])
    for g in range(heads // GROUP):
        lanes = slice(g * GROUP * size, (g + 1) * GROUP * size)
        q4 = dot_nn(flat, wq[:, lanes]).astype(BF16)
        k4 = dot_nn(flat, wk[:, lanes]).astype(BF16)
        for h in range(GROUP):
            q_out[g * GROUP + h] = gather_head(q4, seqs, h, size)
            k_out[g * GROUP + h] = gather_head(k4, seqs, h, size)


def first_sum_kernel(radix, keep, recv, own_out, *outs):
    for m, out in zip(range(radix), (own_out,) + outs):
        total = keep[m].astype(F32) + recv[m].astype(F32)
        out[...] = total.astype(out.dtype)


def sum_kernel(radix, count, keep, *refs):
    terms, own_out, outs = refs[: count - 1], refs[count - 1], refs[count:]
    assert len(outs) == radix - 1
    for m, out in enumerate((own_out,) + outs):
        total = keep[m]
        for t in terms:
            total = total + t[m].astype(F32)
        out[...] = total.astype(out.dtype)


def softmax_kernel(p_rows, keep, *refs):
    terms, out = refs[:-1], refs[-1]
    total = keep[...]
    for t in terms:
        total = total + t[...].astype(F32)
    p = p_rows[...]
    inner = jnp.sum(p * total, axis=-1, keepdims=True)
    out[...] = (p * (total - inner)).astype(BF16)


def post_kernel(dims, radices, chunk, last, sc, *refs):
    seqs, length, _, size, cores, others, rows = dims
    first_head, count = chunk
    first = radices[0]
    own, other = refs[:first], refs[first : 2 * first]
    q_all, k_all, w_q, w_k, o_in, out, logit, grads = refs[2 * first : 2 * first + 8]
    scale = (size * seqs * cores * others) ** -0.5
    half = length // cores
    inner = others // first
    for which, parts in ((0, own), (1, other)):
        core = sc[0] if which == 0 else 1 - sc[0]
        for mask in range(others):
            pos = position_of(mask, radices)
            m, rest = pos // inner, pos % inner
            q = sc[1] ^ mask
            start = pl.multiple_of(core * half + q * rows, rows)
            for h in range(count):
                logit[h, pl.ds(start, rows), :] = parts[m][rest, h]
    width = count * size
    for a, b in groups_of(count):
        qs, ks = [], []
        for h in range(a, b):
            lg = logit[h]
            qs.append((scale * dot_nn(lg, k_all[first_head + h])).astype(BF16))
            ks.append((scale * dot_tn(lg, q_all[first_head + h])).astype(BF16))
        for at, parts in ((0, qs), (width, ks)):
            for s, block in enumerate(spread_heads(parts, seqs, size)):
                grads[s * length : (s + 1) * length, at + a * size : at + b * size] = block
    lanes = slice(first_head * size, (first_head + count) * size)
    weights = jnp.concatenate([w_q[:, lanes], w_k[:, lanes]], axis=1)
    if not last:
        out[...] = o_in[...] + dot_nt(grads[...], weights).reshape(out.shape)
        return
    staged, sems = refs[-2:]
    copies = []
    for s in range(seqs):
        staged[s] = o_in[s] + dot_nt(grads[s * length : (s + 1) * length], weights)
        copies.append(pltpu.make_async_copy(staged.at[s], out.at[s], sems.at[s]))
        copies[-1].start()
    for c in copies:
        c.wait()


def head_chunks(heads):
    groups = heads // GROUP
    if groups < 2:
        return ((0, heads),)
    first = max(1, int(groups * FIRST_PART)) * GROUP
    return ((0, first), (first, heads - first))


def exchange(x, axis, mask):
    count = lax.axis_size(axis)
    return lax.ppermute(x, axis, [(i, i ^ mask) for i in range(count)])


def cost(flops, nbytes):
    return pl.CostEstimate(flops=int(flops), bytes_accessed=int(nbytes), transcendentals=0)


def local(inputs, out_grad, w_query, w_key, w_value, w_output, saved_probs):
    seqs, length, width = inputs.shape
    heads = saved_probs.shape[1]
    size = width // heads
    cores, others = lax.axis_size("seqb"), lax.axis_size("seqa")
    rows = length // (cores * others)
    dims = (seqs, length, heads, size, cores, others, rows)
    radices = radices_of(others)
    lanes = seqs * size
    core, chip = lax.axis_index("seqb"), lax.axis_index("seqa")
    sc = jnp.stack([core, chip]).astype(jnp.int32)
    probs = jnp.swapaxes(saved_probs, 0, 1)
    params = pltpu.CompilerParams(vmem_limit_bytes=VMEM_LIMIT)
    proj = 2 * seqs * length * width * width
    mapf = 2 * heads * length * length * lanes
    smem = pl.BlockSpec(memory_space=pltpu.SMEM)
    vmem = pl.BlockSpec(memory_space=pltpu.VMEM)
    hbm = pl.BlockSpec(memory_space=pltpu.HBM)
    m_shape = lambda n: jax.ShapeDtypeStruct((others, n, rows, length), BF16)
    v_shape = lambda n: jax.ShapeDtypeStruct((n, length, lanes), BF16)
    like = lambda a: jax.ShapeDtypeStruct(a.shape, a.dtype)
    total_shape = jax.ShapeDtypeStruct(inputs.shape, F32)
    chunks = head_chunks(heads)

    def kernel(body, in_specs, outs, flops, nbytes, limit=VMEM_LIMIT, **more):
        specs = more.pop("out_specs", [vmem] * len(outs))
        return pl.pallas_call(
            body,
            in_specs=in_specs,
            out_specs=specs,
            out_shape=outs,
            compiler_params=pltpu.CompilerParams(vmem_limit_bytes=limit),
            cost_estimate=cost(flops, nbytes),
            **more,
        )

    a_alls, keeps, recvs = [], [], []
    for c, (first, n) in enumerate(chunks):
        share = n / heads
        if c == 0:
            in_hbm = [
                pltpu.with_memory_space_constraint(a, pltpu.HBM)
                for a in (inputs, w_value, out_grad, w_output)
            ]
            m_send, a_all, v_all, x_in, og_in, wo_in, wv_in = kernel(
                functools.partial(first_map_kernel, dims, radices),
                [smem, hbm, hbm, hbm, hbm],
                [m_shape(n), v_shape(n), v_shape(n), like(inputs), like(out_grad)]
                + [like(w_output), like(w_value)],
                share * (2 * proj + mapf / 2),
                8e6,
                scratch_shapes=[pltpu.SemaphoreType.DMA((4,))],
            )(sc, *in_hbm)
        else:
            m_send, a_all, v_all = kernel(
                functools.partial(map_send_kernel, dims, radices, first),
                [smem] + [vmem] * 4,
                [m_shape(n), v_shape(n), v_shape(n)],
                share * (2 * proj + mapf / 2),
                2e6,
            )(sc, x_in, wv_in, og_in, wo_in)
        recvs.append(exchange(m_send, "seqb", 1))
        keeps += kernel(
            functools.partial(map_keep_kernel, dims, radices),
            [smem, vmem, vmem],
            [m_shape(n)],
            share * mapf / 2,
            2e6,
        )(sc, a_all, v_all)
        a_alls.append(a_all)

    o_v, *p_rows = kernel(
        functools.partial(value_kernel, dims, chunks),
        [smem] + [vmem] * (len(chunks) + 2),
        [total_shape] + [jax.ShapeDtypeStruct((n, rows, length), F32) for _, n in chunks],
        proj + mapf,
        8e6,
        scratch_shapes=[pltpu.VMEM((seqs * length, width), BF16)],
    )(sc, *a_alls, wv_in, probs)
    q_all, k_all = kernel(
        functools.partial(query_key_kernel, dims),
        [vmem] * 3,
        [v_shape(heads), v_shape(heads)],
        2 * proj,
        6e6,
    )(x_in, w_query, w_key)

    small = lambda body, outs, count: kernel(body, [vmem] * count, outs, 1e6, 1e6, limit=6 << 20)
    logits = []
    for c, (first, n) in enumerate(chunks):
        shape = lambda k: radices[k:] + (n, rows, length)
        split = lambda k: [jax.ShapeDtypeStruct(shape(k + 1), F32)] + [
            jax.ShapeDtypeStruct(shape(k + 1), BF16)
        ] * (radices[k] - 1)
        keep, *sends = small(
            functools.partial(first_sum_kernel, radices[0]), split(0), 2
        )(keeps[c].reshape(shape(0)), recvs[c].reshape(shape(0)))
        shift = 0
        for k, r in enumerate(radices):
            terms = [exchange(x, "seqa", m << shift) for m, x in enumerate(sends, 1)]
            shift += r.bit_length() - 1
            if k + 1 < len(radices):
                keep, *sends = small(
                    functools.partial(sum_kernel, radices[k + 1], r), split(k + 1), r
                )(keep, *terms)
        logits += small(
            softmax_kernel, [jax.ShapeDtypeStruct((n, rows, length), BF16)], len(terms) + 2
        )(p_rows[c], keep, *terms)

    total = o_v
    for c, (first, n) in enumerate(chunks):
        last = c + 1 == len(chunks)
        parts = [logits[c]]
        shift = others.bit_length() - 1
        for k, r in list(enumerate(radices))[::-1]:
            block = jnp.stack(parts) if len(parts) > 1 else parts[0][None]
            if block.ndim > 4:
                block = block.reshape((-1,) + block.shape[2:])
            shift -= r.bit_length() - 1
            parts = [block] + [exchange(block, "seqa", m << shift) for m in range(1, r)]
        crossed = [exchange(p, "seqb", 1) for p in parts]
        total = kernel(
            functools.partial(post_kernel, dims, radices, chunks[c], last),
            [smem] + [vmem] * (2 * radices[0] + 5),
            total_shape,
            n / heads * (2 * proj + 2 * mapf),
            4e6,
            out_specs=hbm if last else vmem,
            scratch_shapes=[
                pltpu.VMEM((n, length, length), BF16),
                pltpu.VMEM((seqs * length, 2 * n * size), BF16),
            ]
            + (
                [pltpu.VMEM((seqs, length, width), F32), pltpu.SemaphoreType.DMA((seqs,))]
                if last
                else []
            ),
        )(sc, *parts, *crossed, q_all, k_all, w_query, w_key, total)
    return total


def solution(mesh):
    placed = (
        P(("grp", "seqa", "seqb"), None, None),
        P(("grp", "seqa", "seqb"), None, None),
        P(),
        P(),
        P(),
        P(),
        P("grp", None, None),
    )

    return jax.shard_map(
        local,
        mesh=mesh,
        in_specs=placed,
        out_specs=P(("grp", "seqa", "seqb"), None, None),
        check_vma=False,
    )
```

```python
import functools

import jax
import jax.numpy as jnp
from jax import lax
from jax.experimental import pallas as pl
from jax.experimental.pallas import tpu as pltpu
from jax.sharding import PartitionSpec as P


F32 = jnp.float32
BF16 = jnp.bfloat16
VMEM_LIMIT = 14 << 20
FIRST_PART = 0.67
GROUP = 4


def dot_nn(a, b):
    return lax.dot_general(a, b, (((1,), (0,)), ((), ())), preferred_element_type=F32)


def dot_nt(a, b):
    return lax.dot_general(a, b, (((1,), (1,)), ((), ())), preferred_element_type=F32)


def dot_tn(a, b):
    return lax.dot_general(a, b, (((0,), (0,)), ((), ())), preferred_element_type=F32)


def gather_head(rows, seqs, head, size):
    n = rows.shape[0] // seqs
    lanes = slice(head * size, (head + 1) * size)
    return jnp.concatenate([rows[s * n : (s + 1) * n, lanes] for s in range(seqs)], axis=1)


def spread_heads(parts, seqs, size):
    return [
        jnp.concatenate([p[:, s * size : (s + 1) * size] for p in parts], axis=1)
        for s in range(seqs)
    ]


def radices_of(count):
    out = []
    while count > 1:
        r = 4 if count % 4 == 0 else 2
        assert count % r == 0
        out.append(r)
        count //= r
    return tuple(out)


def position_of(mask, radices):
    pos, shift = 0, 0
    for r in radices:
        bits = r.bit_length() - 1
        pos = pos * r + ((mask >> shift) & (r - 1))
        shift += bits
    return pos


def fetch(pairs, sems):
    copies = [pltpu.make_async_copy(a, b, sems.at[i]) for i, (a, b) in enumerate(pairs)]
    for c in copies:
        c.start()
    return copies


def store_map(m, h, m_out, chip, others, rows, radices):
    for q in range(others):
        m_out[position_of(chip ^ q, radices), h] = m[q * rows : (q + 1) * rows]


def groups_of(count):
    return [(g, min(g + GROUP, count)) for g in range(0, count, GROUP)]


def value_rows(x, wv, v_out, first, dims):
    seqs, length, _, size, _, _, _ = dims
    flat = x[...].reshape(seqs * length, x.shape[-1])
    for a, b in groups_of(v_out.shape[0]):
        v4 = dot_nn(flat, wv[:, (first + a) * size : (first + b) * size]).astype(BF16)
        for h in range(b - a):
            v_out[a + h] = gather_head(v4, seqs, h, size)


def attn_rows(og, wo, a_out, first, dims):
    seqs, length, _, size, _, _, _ = dims
    flat = og[...].reshape(seqs * length, og.shape[-1])
    for a, b in groups_of(a_out.shape[0]):
        a4 = dot_nt(flat, wo[(first + a) * size : (first + b) * size]).astype(BF16)
        for h in range(b - a):
            a_out[a + h] = gather_head(a4, seqs, h, size)


def map_rows(core, chip, a_all, v_all, m_out, dims, radices):
    _, length, _, _, cores, others, rows = dims
    half = length // cores
    start = pl.multiple_of(core * half, half)
    for h in range(v_all.shape[0]):
        m = dot_nt(a_all[h, pl.ds(start, half), :], v_all[h]).astype(BF16)
        store_map(m, h, m_out, chip, others, rows, radices)


def first_map_kernel(
    dims, radices, sc, x_hbm, wv_hbm, og_hbm, wo_hbm, m_out, a_out, v_out, x, og, wo, wv, sems
):
    seqs, length, _, size = dims[:4]
    used = pl.ds(0, v_out.shape[0] * size)
    rest = pl.ds(v_out.shape[0] * size, wv.shape[1] - v_out.shape[0] * size)
    pair = seqs // 2
    halves = [pl.ds(0, pair), pl.ds(pair, seqs - pair)]
    copies = fetch(
        [(wv_hbm.at[:, used], wv.at[:, used])]
        + [(x_hbm.at[part], x.at[part]) for part in halves]
        + [(wo_hbm, wo), (og_hbm, og), (wv_hbm.at[:, rest], wv.at[:, rest])],
        sems,
    )
    copies[0].wait()
    for p, part in enumerate(halves):
        copies[1 + p].wait()
        count = seqs - pair if p else pair
        flat = x[part].reshape(count * length, x.shape[-1])
        at = p * pair * size
        for a, b in groups_of(v_out.shape[0]):
            v4 = dot_nn(flat, wv[:, a * size : b * size]).astype(BF16)
            for h in range(b - a):
                v_out[a + h, :, at : at + count * size] = gather_head(v4, count, h, size)
    copies[3].wait()
    copies[4].wait()
    attn_rows(og, wo, a_out, 0, dims)
    map_rows(1 - sc[0], sc[1], a_out, v_out, m_out, dims, radices)
    copies[5].wait()


def map_send_kernel(dims, radices, first, sc, x, wv, og, wo, m_out, a_out, v_out):
    value_rows(x, wv, v_out, first, dims)
    attn_rows(og, wo, a_out, first, dims)
    map_rows(1 - sc[0], sc[1], a_out, v_out, m_out, dims, radices)


def map_keep_kernel(dims, radices, sc, a_all, v_all, m_out):
    map_rows(sc[0], sc[1], a_all, v_all, m_out, dims, radices)


def value_kernel(dims, chunks, sc, *refs):
    seqs, length, _, size, _, others, rows = dims
    a_refs, (wv, probs, o_out), p_outs = (
        refs[: len(chunks)],
        refs[len(chunks) : len(chunks) + 3],
        refs[len(chunks) + 3 : -1],
    )
    v_grad = refs[-1]
    mine = pl.ds(pl.multiple_of((sc[0] * others + sc[1]) * rows, rows), rows)
    for (first, n), a_all, p_out in zip(chunks, a_refs, p_outs):
        p_out[...] = probs[first : first + n, mine, :]
        for a, b in groups_of(n):
            parts = [
                dot_tn(probs[first + h].astype(BF16), a_all[h]).astype(BF16)
                for h in range(a, b)
            ]
            lanes = slice((first + a) * size, (first + b) * size)
            for s, block in enumerate(spread_heads(parts, seqs, size)):
                v_grad[s * length : (s + 1) * length, lanes] = block
    o_out[...] = dot_nt(v_grad[...], wv[...]).reshape(o_out.shape)


def query_key_kernel(dims, x, wq, wk, q_out, k_out):
    seqs, length, heads, size, _, _, _ = dims
    flat = x[...].reshape(seqs * length, x.shape[-1])
    for g in range(heads // GROUP):
        lanes = slice(g * GROUP * size, (g + 1) * GROUP * size)
        q4 = dot_nn(flat, wq[:, lanes]).astype(BF16)
        k4 = dot_nn(flat, wk[:, lanes]).astype(BF16)
        for h in range(GROUP):
            q_out[g * GROUP + h] = gather_head(q4, seqs, h, size)
            k_out[g * GROUP + h] = gather_head(k4, seqs, h, size)


def first_sum_kernel(radix, keep, recv, own_out, *outs):
    for m, out in zip(range(radix), (own_out,) + outs):
        total = keep[m].astype(F32) + recv[m].astype(F32)
        out[...] = total.astype(out.dtype)


def sum_kernel(radix, count, keep, *refs):
    terms, own_out, outs = refs[: count - 1], refs[count - 1], refs[count:]
    assert len(outs) == radix - 1
    for m, out in enumerate((own_out,) + outs):
        total = keep[m]
        for t in terms:
            total = total + t[m].astype(F32)
        out[...] = total.astype(out.dtype)


def softmax_kernel(p_rows, keep, *refs):
    terms, out = refs[:-1], refs[-1]
    total = keep[...]
    for t in terms:
        total = total + t[...].astype(F32)
    p = p_rows[...]
    inner = jnp.sum(p * total, axis=-1, keepdims=True)
    out[...] = (p * (total - inner)).astype(BF16)


def post_kernel(dims, radices, chunk, last, sc, *refs):
    seqs, length, _, size, cores, others, rows = dims
    first_head, count = chunk
    first = radices[0]
    own, other = refs[:first], refs[first : 2 * first]
    if last:
        q_all, k_all, w_q, w_k, o_in, out, logit, grads, staged, sems = refs[2 * first :]
    else:
        q_all, k_all, grads, logit = refs[2 * first :]
    scale = (size * seqs * cores * others) ** -0.5
    half = length // cores
    inner = others // first
    for which, parts in ((0, own), (1, other)):
        core = sc[0] if which == 0 else 1 - sc[0]
        for mask in range(others):
            pos = position_of(mask, radices)
            m, rest = pos // inner, pos % inner
            q = sc[1] ^ mask
            start = pl.multiple_of(core * half + q * rows, rows)
            for h in range(count):
                logit[h, pl.ds(start, rows), :] = parts[m][rest, h]
    width = count * size
    for a, b in groups_of(count):
        qs, ks = [], []
        for h in range(a, b):
            lg = logit[h]
            qs.append((scale * dot_nn(lg, k_all[first_head + h])).astype(BF16))
            ks.append((scale * dot_tn(lg, q_all[first_head + h])).astype(BF16))
        for at, parts in ((0, qs), (width, ks)):
            for s, block in enumerate(spread_heads(parts, seqs, size)):
                grads[s * length : (s + 1) * length, at + a * size : at + b * size] = block
    if not last:
        return
    weights = both_weights(w_q, w_k, first_head, count, size)
    copies = []
    for s in range(seqs):
        staged[s] = o_in[s] + dot_nt(grads[s * length : (s + 1) * length], weights)
        copies.append(pltpu.make_async_copy(staged.at[s], out.at[s], sems.at[s]))
        copies[-1].start()
    for c in copies:
        c.wait()


def both_weights(w_q, w_k, first, count, size):
    lanes = slice(first * size, (first + count) * size)
    return jnp.concatenate([w_q[:, lanes], w_k[:, lanes]], axis=1)


def back_kernel(dims, chunk, grads, w_q, w_k, o_in, out):
    weights = both_weights(w_q, w_k, *chunk, dims[3])
    out[...] = o_in[...] + dot_nt(grads[...], weights).reshape(out.shape)


def head_chunks(heads):
    groups = heads // GROUP
    if groups < 2:
        return ((0, heads),)
    first = max(1, int(groups * FIRST_PART)) * GROUP
    return ((0, first), (first, heads - first))


def exchange(x, axis, mask):
    count = lax.axis_size(axis)
    return lax.ppermute(x, axis, [(i, i ^ mask) for i in range(count)])


def cost(flops, nbytes):
    return pl.CostEstimate(flops=int(flops), bytes_accessed=int(nbytes), transcendentals=0)


def local(inputs, out_grad, w_query, w_key, w_value, w_output, saved_probs):
    seqs, length, width = inputs.shape
    heads = saved_probs.shape[1]
    size = width // heads
    cores, others = lax.axis_size("seqb"), lax.axis_size("seqa")
    rows = length // (cores * others)
    dims = (seqs, length, heads, size, cores, others, rows)
    radices = radices_of(others)
    lanes = seqs * size
    core, chip = lax.axis_index("seqb"), lax.axis_index("seqa")
    sc = jnp.stack([core, chip]).astype(jnp.int32)
    probs = jnp.swapaxes(saved_probs, 0, 1)
    params = pltpu.CompilerParams(vmem_limit_bytes=VMEM_LIMIT)
    proj = 2 * seqs * length * width * width
    mapf = 2 * heads * length * length * lanes
    smem = pl.BlockSpec(memory_space=pltpu.SMEM)
    vmem = pl.BlockSpec(memory_space=pltpu.VMEM)
    hbm = pl.BlockSpec(memory_space=pltpu.HBM)
    m_shape = lambda n: jax.ShapeDtypeStruct((others, n, rows, length), BF16)
    v_shape = lambda n: jax.ShapeDtypeStruct((n, length, lanes), BF16)
    like = lambda a: jax.ShapeDtypeStruct(a.shape, a.dtype)
    total_shape = jax.ShapeDtypeStruct(inputs.shape, F32)
    chunks = head_chunks(heads)

    def kernel(body, in_specs, outs, flops, nbytes, limit=VMEM_LIMIT, **more):
        specs = more.pop("out_specs", [vmem] * len(outs))
        return pl.pallas_call(
            body,
            in_specs=in_specs,
            out_specs=specs,
            out_shape=outs,
            compiler_params=pltpu.CompilerParams(vmem_limit_bytes=limit),
            cost_estimate=cost(flops, nbytes),
            **more,
        )

    a_alls, keeps, recvs = [], [], []
    for c, (first, n) in enumerate(chunks):
        share = n / heads
        if c == 0:
            in_hbm = [
                pltpu.with_memory_space_constraint(a, pltpu.HBM)
                for a in (inputs, w_value, out_grad, w_output)
            ]
            m_send, a_all, v_all, x_in, og_in, wo_in, wv_in = kernel(
                functools.partial(first_map_kernel, dims, radices),
                [smem, hbm, hbm, hbm, hbm],
                [m_shape(n), v_shape(n), v_shape(n), like(inputs), like(out_grad)]
                + [like(w_output), like(w_value)],
                share * (2 * proj + mapf / 2),
                8e6,
                scratch_shapes=[pltpu.SemaphoreType.DMA((6,))],
            )(sc, *in_hbm)
        else:
            m_send, a_all, v_all = kernel(
                functools.partial(map_send_kernel, dims, radices, first),
                [smem] + [vmem] * 4,
                [m_shape(n), v_shape(n), v_shape(n)],
                share * (2 * proj + mapf / 2),
                2e6,
            )(sc, x_in, wv_in, og_in, wo_in)
        recvs.append(exchange(m_send, "seqb", 1))
        keeps += kernel(
            functools.partial(map_keep_kernel, dims, radices),
            [smem, vmem, vmem],
            [m_shape(n)],
            share * mapf / 2,
            2e6,
        )(sc, a_all, v_all)
        a_alls.append(a_all)

    o_v, *p_rows = kernel(
        functools.partial(value_kernel, dims, chunks),
        [smem] + [vmem] * (len(chunks) + 2),
        [total_shape] + [jax.ShapeDtypeStruct((n, rows, length), F32) for _, n in chunks],
        proj + mapf,
        8e6,
        scratch_shapes=[pltpu.VMEM((seqs * length, width), BF16)],
    )(sc, *a_alls, wv_in, probs)
    q_all, k_all = kernel(
        functools.partial(query_key_kernel, dims),
        [vmem] * 3,
        [v_shape(heads), v_shape(heads)],
        2 * proj,
        6e6,
    )(x_in, w_query, w_key)

    small = lambda body, outs, count: kernel(body, [vmem] * count, outs, 1e6, 1e6, limit=6 << 20)
    logits = []
    for c, (first, n) in enumerate(chunks):
        shape = lambda k: radices[k:] + (n, rows, length)
        split = lambda k: [jax.ShapeDtypeStruct(shape(k + 1), F32)] + [
            jax.ShapeDtypeStruct(shape(k + 1), BF16)
        ] * (radices[k] - 1)
        keep, *sends = small(
            functools.partial(first_sum_kernel, radices[0]), split(0), 2
        )(keeps[c].reshape(shape(0)), recvs[c].reshape(shape(0)))
        shift = 0
        for k, r in enumerate(radices):
            terms = [exchange(x, "seqa", m << shift) for m, x in enumerate(sends, 1)]
            shift += r.bit_length() - 1
            if k + 1 < len(radices):
                keep, *sends = small(
                    functools.partial(sum_kernel, radices[k + 1], r), split(k + 1), r
                )(keep, *terms)
        logits += small(
            softmax_kernel, [jax.ShapeDtypeStruct((n, rows, length), BF16)], len(terms) + 2
        )(p_rows[c], keep, *terms)

    total = o_v
    for c, (first, n) in enumerate(chunks):
        last = c + 1 == len(chunks)
        parts = [logits[c]]
        shift = others.bit_length() - 1
        for k, r in list(enumerate(radices))[::-1]:
            block = jnp.stack(parts) if len(parts) > 1 else parts[0][None]
            if block.ndim > 4:
                block = block.reshape((-1,) + block.shape[2:])
            shift -= r.bit_length() - 1
            parts = [block] + [exchange(block, "seqa", m << shift) for m in range(1, r)]
        crossed = [exchange(p, "seqb", 1) for p in parts]
        grads_shape = (seqs * length, 2 * n * size)
        logit_scratch = pltpu.VMEM((n, length, length), BF16)
        flops = n / heads * 2 * mapf
        if last:
            total = kernel(
                functools.partial(post_kernel, dims, radices, chunks[c], True),
                [smem] + [vmem] * (2 * radices[0] + 5),
                total_shape,
                n / heads * 2 * proj + flops,
                4e6,
                out_specs=hbm,
                scratch_shapes=[
                    logit_scratch,
                    pltpu.VMEM(grads_shape, BF16),
                    pltpu.VMEM((seqs, length, width), F32),
                    pltpu.SemaphoreType.DMA((seqs,)),
                ],
            )(sc, *parts, *crossed, q_all, k_all, w_query, w_key, total)
        else:
            (grads,) = kernel(
                functools.partial(post_kernel, dims, radices, chunks[c], False),
                [smem] + [vmem] * (2 * radices[0] + 2),
                [jax.ShapeDtypeStruct(grads_shape, BF16)],
                flops,
                4e6,
                scratch_shapes=[logit_scratch],
            )(sc, *parts, *crossed, q_all, k_all)
            (total,) = kernel(
                functools.partial(back_kernel, dims, chunks[c]),
                [vmem] * 4,
                [total_shape],
                n / heads * 2 * proj,
                6e6,
            )(grads, w_query, w_key, total)
    return total


def solution(mesh):
    placed = (
        P(("grp", "seqa", "seqb"), None, None),
        P(("grp", "seqa", "seqb"), None, None),
        P(),
        P(),
        P(),
        P(),
        P("grp", None, None),
    )

    return jax.shard_map(
        local,
        mesh=mesh,
        in_specs=placed,
        out_specs=P(("grp", "seqa", "seqb"), None, None),
        check_vma=False,
    )
```

```python
import functools

import jax
import jax.numpy as jnp
from jax import lax
from jax.experimental import pallas as pl
from jax.experimental.pallas import tpu as pltpu
from jax.sharding import PartitionSpec as P


F32 = jnp.float32
BF16 = jnp.bfloat16
VMEM_LIMIT = 14 << 20
FIRST_PART = 0.67
GROUP = 4


def dot_nn(a, b):
    return lax.dot_general(a, b, (((1,), (0,)), ((), ())), preferred_element_type=F32)


def dot_nt(a, b):
    return lax.dot_general(a, b, (((1,), (1,)), ((), ())), preferred_element_type=F32)


def dot_tn(a, b):
    return lax.dot_general(a, b, (((0,), (0,)), ((), ())), preferred_element_type=F32)


def gather_head(rows, seqs, head, size):
    n = rows.shape[0] // seqs
    lanes = slice(head * size, (head + 1) * size)
    return jnp.concatenate([rows[s * n : (s + 1) * n, lanes] for s in range(seqs)], axis=1)


def spread_heads(parts, seqs, size):
    return [
        jnp.concatenate([p[:, s * size : (s + 1) * size] for p in parts], axis=1)
        for s in range(seqs)
    ]


def radices_of(count):
    out = []
    while count > 1:
        r = 4 if count % 4 == 0 else 2
        assert count % r == 0
        out.append(r)
        count //= r
    return tuple(out)


def position_of(mask, radices):
    pos, shift = 0, 0
    for r in radices:
        bits = r.bit_length() - 1
        pos = pos * r + ((mask >> shift) & (r - 1))
        shift += bits
    return pos


def fetch(pairs, sems):
    copies = [pltpu.make_async_copy(a, b, sems.at[i]) for i, (a, b) in enumerate(pairs)]
    for c in copies:
        c.start()
    return copies


def store_map(m, h, m_out, chip, others, rows, radices):
    for q in range(others):
        m_out[position_of(chip ^ q, radices), h] = m[q * rows : (q + 1) * rows]


def groups_of(count):
    return [(g, min(g + GROUP, count)) for g in range(0, count, GROUP)]


def value_rows(x, wv, v_out, first, dims):
    seqs, length, _, size, _, _, _ = dims
    flat = x[...].reshape(seqs * length, x.shape[-1])
    for a, b in groups_of(v_out.shape[0]):
        v4 = dot_nn(flat, wv[:, (first + a) * size : (first + b) * size]).astype(BF16)
        for h in range(b - a):
            v_out[a + h] = gather_head(v4, seqs, h, size)


def attn_rows(og, wo, a_out, first, dims):
    seqs, length, _, size, _, _, _ = dims
    flat = og[...].reshape(seqs * length, og.shape[-1])
    for a, b in groups_of(a_out.shape[0]):
        a4 = dot_nt(flat, wo[(first + a) * size : (first + b) * size]).astype(BF16)
        for h in range(b - a):
            a_out[a + h] = gather_head(a4, seqs, h, size)


def map_rows(core, chip, a_all, v_all, m_out, dims, radices):
    _, length, _, _, cores, others, rows = dims
    half = length // cores
    start = pl.multiple_of(core * half, half)
    for h in range(v_all.shape[0]):
        m = dot_nt(a_all[h, pl.ds(start, half), :], v_all[h]).astype(BF16)
        store_map(m, h, m_out, chip, others, rows, radices)


def first_map_kernel(
    dims, radices, sc, x_hbm, wv_hbm, og_hbm, wo_hbm, m_out, a_out, v_out, x, og, wo, wv, sems
):
    seqs, length, _, size = dims[:4]
    used = pl.ds(0, v_out.shape[0] * size)
    rest = pl.ds(v_out.shape[0] * size, wv.shape[1] - v_out.shape[0] * size)
    pair = seqs // 2
    halves = [pl.ds(0, pair), pl.ds(pair, seqs - pair)]
    copies = fetch(
        [(wv_hbm.at[:, used], wv.at[:, used])]
        + [(x_hbm.at[part], x.at[part]) for part in halves]
        + [(wo_hbm, wo), (og_hbm, og), (wv_hbm.at[:, rest], wv.at[:, rest])],
        sems,
    )
    copies[0].wait()
    for p, part in enumerate(halves):
        copies[1 + p].wait()
        count = seqs - pair if p else pair
        flat = x[part].reshape(count * length, x.shape[-1])
        at = p * pair * size
        for a, b in groups_of(v_out.shape[0]):
            v4 = dot_nn(flat, wv[:, a * size : b * size]).astype(BF16)
            for h in range(b - a):
                v_out[a + h, :, at : at + count * size] = gather_head(v4, count, h, size)
    copies[3].wait()
    copies[4].wait()
    attn_rows(og, wo, a_out, 0, dims)
    map_rows(1 - sc[0], sc[1], a_out, v_out, m_out, dims, radices)
    copies[5].wait()


def map_send_kernel(dims, radices, first, sc, v_all, og, wo, m_out, a_out):
    attn_rows(og, wo, a_out, first, dims)
    map_rows(1 - sc[0], sc[1], a_out, v_all, m_out, dims, radices)


def map_keep_kernel(dims, radices, sc, a_all, v_all, m_out):
    map_rows(sc[0], sc[1], a_all, v_all, m_out, dims, radices)


def first_keep_kernel(dims, radices, following, sc, a_all, v_all, x, wv, m_out, v_next):
    map_rows(sc[0], sc[1], a_all, v_all, m_out, dims, radices)
    value_rows(x, wv, v_next, following, dims)


def value_kernel(dims, chunks, sc, *refs):
    seqs, length, _, size, _, others, rows = dims
    a_refs, (wv, probs, o_out), p_outs = (
        refs[: len(chunks)],
        refs[len(chunks) : len(chunks) + 3],
        refs[len(chunks) + 3 : -1],
    )
    v_grad = refs[-1]
    mine = pl.ds(pl.multiple_of((sc[0] * others + sc[1]) * rows, rows), rows)
    for (first, n), a_all, p_out in zip(chunks, a_refs, p_outs):
        p_out[...] = probs[first : first + n, mine, :]
        for a, b in groups_of(n):
            parts = [
                dot_tn(probs[first + h].astype(BF16), a_all[h]).astype(BF16)
                for h in range(a, b)
            ]
            lanes = slice((first + a) * size, (first + b) * size)
            for s, block in enumerate(spread_heads(parts, seqs, size)):
                v_grad[s * length : (s + 1) * length, lanes] = block
    o_out[...] = dot_nt(v_grad[...], wv[...]).reshape(o_out.shape)


def query_key_kernel(dims, x, wq, wk, q_out, k_out):
    seqs, length, heads, size, _, _, _ = dims
    flat = x[...].reshape(seqs * length, x.shape[-1])
    for g in range(heads // GROUP):
        lanes = slice(g * GROUP * size, (g + 1) * GROUP * size)
        q4 = dot_nn(flat, wq[:, lanes]).astype(BF16)
        k4 = dot_nn(flat, wk[:, lanes]).astype(BF16)
        for h in range(GROUP):
            q_out[g * GROUP + h] = gather_head(q4, seqs, h, size)
            k_out[g * GROUP + h] = gather_head(k4, seqs, h, size)


def first_sum_kernel(radix, keep, recv, own_out, *outs):
    for m, out in zip(range(radix), (own_out,) + outs):
        total = keep[m].astype(F32) + recv[m].astype(F32)
        out[...] = total.astype(out.dtype)


def sum_kernel(radix, count, keep, *refs):
    terms, own_out, outs = refs[: count - 1], refs[count - 1], refs[count:]
    assert len(outs) == radix - 1
    for m, out in enumerate((own_out,) + outs):
        total = keep[m]
        for t in terms:
            total = total + t[m].astype(F32)
        out[...] = total.astype(out.dtype)


def softmax_kernel(p_rows, keep, *refs):
    terms, out = refs[:-1], refs[-1]
    total = keep[...]
    for t in terms:
        total = total + t[...].astype(F32)
    p = p_rows[...]
    inner = jnp.sum(p * total, axis=-1, keepdims=True)
    out[...] = (p * (total - inner)).astype(BF16)


def post_kernel(dims, radices, chunk, last, sc, *refs):
    seqs, length, _, size, cores, others, rows = dims
    first_head, count = chunk
    first = radices[0]
    own, other = refs[:first], refs[first : 2 * first]
    if last:
        q_all, k_all, w_q, w_k, o_in, out, logit, grads, staged, sems = refs[2 * first :]
    else:
        q_all, k_all, grads, logit = refs[2 * first :]
    scale = (size * seqs * cores * others) ** -0.5
    half = length // cores
    inner = others // first
    for which, parts in ((0, own), (1, other)):
        core = sc[0] if which == 0 else 1 - sc[0]
        for mask in range(others):
            pos = position_of(mask, radices)
            m, rest = pos // inner, pos % inner
            q = sc[1] ^ mask
            start = pl.multiple_of(core * half + q * rows, rows)
            for h in range(count):
                logit[h, pl.ds(start, rows), :] = parts[m][rest, h]
    width = count * size
    for a, b in groups_of(count):
        qs, ks = [], []
        for h in range(a, b):
            lg = logit[h]
            qs.append((scale * dot_nn(lg, k_all[first_head + h])).astype(BF16))
            ks.append((scale * dot_tn(lg, q_all[first_head + h])).astype(BF16))
        for at, parts in ((0, qs), (width, ks)):
            for s, block in enumerate(spread_heads(parts, seqs, size)):
                grads[s * length : (s + 1) * length, at + a * size : at + b * size] = block
    if not last:
        return
    weights = both_weights(w_q, w_k, first_head, count, size)
    copies = []
    for s in range(seqs):
        staged[s] = o_in[s] + dot_nt(grads[s * length : (s + 1) * length], weights)
        copies.append(pltpu.make_async_copy(staged.at[s], out.at[s], sems.at[s]))
        copies[-1].start()
    for c in copies:
        c.wait()


def both_weights(w_q, w_k, first, count, size):
    lanes = slice(first * size, (first + count) * size)
    return jnp.concatenate([w_q[:, lanes], w_k[:, lanes]], axis=1)


def back_kernel(dims, chunk, grads, w_q, w_k, o_in, out):
    weights = both_weights(w_q, w_k, *chunk, dims[3])
    out[...] = o_in[...] + dot_nt(grads[...], weights).reshape(out.shape)


def head_chunks(heads):
    groups = heads // GROUP
    if groups < 2:
        return ((0, heads),)
    first = max(1, int(groups * FIRST_PART)) * GROUP
    return ((0, first), (first, heads - first))


def exchange(x, axis, mask):
    count = lax.axis_size(axis)
    return lax.ppermute(x, axis, [(i, i ^ mask) for i in range(count)])


def cost(flops, nbytes):
    return pl.CostEstimate(flops=int(flops), bytes_accessed=int(nbytes), transcendentals=0)


def local(inputs, out_grad, w_query, w_key, w_value, w_output, saved_probs):
    seqs, length, width = inputs.shape
    heads = saved_probs.shape[1]
    size = width // heads
    cores, others = lax.axis_size("seqb"), lax.axis_size("seqa")
    rows = length // (cores * others)
    dims = (seqs, length, heads, size, cores, others, rows)
    radices = radices_of(others)
    lanes = seqs * size
    core, chip = lax.axis_index("seqb"), lax.axis_index("seqa")
    sc = jnp.stack([core, chip]).astype(jnp.int32)
    probs = jnp.swapaxes(saved_probs, 0, 1)
    params = pltpu.CompilerParams(vmem_limit_bytes=VMEM_LIMIT)
    proj = 2 * seqs * length * width * width
    mapf = 2 * heads * length * length * lanes
    smem = pl.BlockSpec(memory_space=pltpu.SMEM)
    vmem = pl.BlockSpec(memory_space=pltpu.VMEM)
    hbm = pl.BlockSpec(memory_space=pltpu.HBM)
    m_shape = lambda n: jax.ShapeDtypeStruct((others, n, rows, length), BF16)
    v_shape = lambda n: jax.ShapeDtypeStruct((n, length, lanes), BF16)
    like = lambda a: jax.ShapeDtypeStruct(a.shape, a.dtype)
    total_shape = jax.ShapeDtypeStruct(inputs.shape, F32)
    chunks = head_chunks(heads)

    def kernel(body, in_specs, outs, flops, nbytes, limit=VMEM_LIMIT, **more):
        specs = more.pop("out_specs", [vmem] * len(outs))
        return pl.pallas_call(
            body,
            in_specs=in_specs,
            out_specs=specs,
            out_shape=outs,
            compiler_params=pltpu.CompilerParams(vmem_limit_bytes=limit),
            cost_estimate=cost(flops, nbytes),
            **more,
        )

    a_alls, keeps, recvs = [], [], []
    for c, (first, n) in enumerate(chunks):
        share = n / heads
        if c == 0:
            in_hbm = [
                pltpu.with_memory_space_constraint(a, pltpu.HBM)
                for a in (inputs, w_value, out_grad, w_output)
            ]
            m_send, a_all, v_all, x_in, og_in, wo_in, wv_in = kernel(
                functools.partial(first_map_kernel, dims, radices),
                [smem, hbm, hbm, hbm, hbm],
                [m_shape(n), v_shape(n), v_shape(n), like(inputs), like(out_grad)]
                + [like(w_output), like(w_value)],
                share * (2 * proj + mapf / 2),
                8e6,
                scratch_shapes=[pltpu.SemaphoreType.DMA((6,))],
            )(sc, *in_hbm)
        else:
            v_all = v_next
            m_send, a_all = kernel(
                functools.partial(map_send_kernel, dims, radices, first),
                [smem] + [vmem] * 3,
                [m_shape(n), v_shape(n)],
                share * (proj + mapf / 2),
                2e6,
            )(sc, v_all, og_in, wo_in)
        recvs.append(exchange(m_send, "seqb", 1))
        if c == 0:
            following, count = chunks[1]
            m_keep, v_next = kernel(
                functools.partial(first_keep_kernel, dims, radices, following),
                [smem] + [vmem] * 4,
                [m_shape(n), v_shape(count)],
                share * mapf / 2 + proj * count / heads,
                3e6,
            )(sc, a_all, v_all, x_in, wv_in)
        else:
            (m_keep,) = kernel(
                functools.partial(map_keep_kernel, dims, radices),
                [smem, vmem, vmem],
                [m_shape(n)],
                share * mapf / 2,
                2e6,
            )(sc, a_all, v_all)
        keeps.append(m_keep)
        a_alls.append(a_all)

    o_v, *p_rows = kernel(
        functools.partial(value_kernel, dims, chunks),
        [smem] + [vmem] * (len(chunks) + 2),
        [total_shape] + [jax.ShapeDtypeStruct((n, rows, length), F32) for _, n in chunks],
        proj + mapf,
        8e6,
        scratch_shapes=[pltpu.VMEM((seqs * length, width), BF16)],
    )(sc, *a_alls, wv_in, probs)
    q_all, k_all = kernel(
        functools.partial(query_key_kernel, dims),
        [vmem] * 3,
        [v_shape(heads), v_shape(heads)],
        2 * proj,
        6e6,
    )(x_in, w_query, w_key)

    small = lambda body, outs, count: kernel(body, [vmem] * count, outs, 1e6, 1e6, limit=6 << 20)
    logits = []
    for c, (first, n) in enumerate(chunks):
        shape = lambda k: radices[k:] + (n, rows, length)
        split = lambda k: [jax.ShapeDtypeStruct(shape(k + 1), F32)] + [
            jax.ShapeDtypeStruct(shape(k + 1), BF16)
        ] * (radices[k] - 1)
        keep, *sends = small(
            functools.partial(first_sum_kernel, radices[0]), split(0), 2
        )(keeps[c].reshape(shape(0)), recvs[c].reshape(shape(0)))
        shift = 0
        for k, r in enumerate(radices):
            terms = [exchange(x, "seqa", m << shift) for m, x in enumerate(sends, 1)]
            shift += r.bit_length() - 1
            if k + 1 < len(radices):
                keep, *sends = small(
                    functools.partial(sum_kernel, radices[k + 1], r), split(k + 1), r
                )(keep, *terms)
        logits += small(
            softmax_kernel, [jax.ShapeDtypeStruct((n, rows, length), BF16)], len(terms) + 2
        )(p_rows[c], keep, *terms)

    total = o_v
    for c, (first, n) in enumerate(chunks):
        last = c + 1 == len(chunks)
        parts = [logits[c]]
        shift = others.bit_length() - 1
        for k, r in list(enumerate(radices))[::-1]:
            block = jnp.stack(parts) if len(parts) > 1 else parts[0][None]
            if block.ndim > 4:
                block = block.reshape((-1,) + block.shape[2:])
            shift -= r.bit_length() - 1
            parts = [block] + [exchange(block, "seqa", m << shift) for m in range(1, r)]
        crossed = [exchange(p, "seqb", 1) for p in parts]
        grads_shape = (seqs * length, 2 * n * size)
        logit_scratch = pltpu.VMEM((n, length, length), BF16)
        flops = n / heads * 2 * mapf
        if last:
            total = kernel(
                functools.partial(post_kernel, dims, radices, chunks[c], True),
                [smem] + [vmem] * (2 * radices[0] + 5),
                total_shape,
                n / heads * 2 * proj + flops,
                4e6,
                out_specs=hbm,
                scratch_shapes=[
                    logit_scratch,
                    pltpu.VMEM(grads_shape, BF16),
                    pltpu.VMEM((seqs, length, width), F32),
                    pltpu.SemaphoreType.DMA((seqs,)),
                ],
            )(sc, *parts, *crossed, q_all, k_all, w_query, w_key, total)
        else:
            (grads,) = kernel(
                functools.partial(post_kernel, dims, radices, chunks[c], False),
                [smem] + [vmem] * (2 * radices[0] + 2),
                [jax.ShapeDtypeStruct(grads_shape, BF16)],
                flops,
                4e6,
                scratch_shapes=[logit_scratch],
            )(sc, *parts, *crossed, q_all, k_all)
            (total,) = kernel(
                functools.partial(back_kernel, dims, chunks[c]),
                [vmem] * 4,
                [total_shape],
                n / heads * 2 * proj,
                6e6,
            )(grads, w_query, w_key, total)
    return total


def solution(mesh):
    placed = (
        P(("grp", "seqa", "seqb"), None, None),
        P(("grp", "seqa", "seqb"), None, None),
        P(),
        P(),
        P(),
        P(),
        P("grp", None, None),
    )

    return jax.shard_map(
        local,
        mesh=mesh,
        in_specs=placed,
        out_specs=P(("grp", "seqa", "seqb"), None, None),
        check_vma=False,
    )
```
